32 devices in a mesh: rep: 2 (over y), hid: 8 (over z, x), wid: 2 (over core).
Axes of the slice: x: 2, y: 2, z: 4, core: 2. Of those that a mesh axis runs over, the one named last changes fastest.
Arguments:
- states: float32 [32, 8192], P(('rep', 'hid'), 'wid'), parts along dimension 0, may hold values from -6 to 6
- norm_gain: float32 [8192], P('wid'), may hold values from 0.25 to 1.75
- gate_weight: bfloat16 [8192, 16384], P('wid', 'hid'), may hold values from -0.0625 to 0.0625
- up_weight: bfloat16 [8192, 16384], P('wid', 'hid'), may hold values from -0.0625 to 0.0625
- down_weight: bfloat16 [16384, 8192], P('hid', 'wid'), may hold values from -0.046875 to 0.046875
Outputs:
- updated: float32 [32, 8192], P(('rep', 'hid'), 'wid'), parts along dimension 0
The draws below stay inside these ranges and needn't reach their ends.
There are 2 independent parts, one for each index of `rep`. The reference program is written for one: setup_inputs(seed, part) draws one part's arguments, and reference() takes and returns one part's arrays. A program takes and returns all parts, laid end to end along the dimension named above; an argument that names none is the same for every part. Nothing has to cross between parts.
All inputs are finite; a program needn't handle non-finite values.
Results may differ from the reference program's by a relative error of at most 0.0029.
Values may be sent and summed in bfloat16 or wider, within the bound.
A program may use at most 128 MiB of HBM per device.

```python
import jax
import jax.numpy as jnp
from jax import lax

D = 8192
FF = 16384
STREAMS = 16


def steps_of(key, extent, shards, least, high):
    def one(position, shards_of):
        draws = jax.random.uniform(jax.random.fold_in(jax.random.fold_in(key, 6), position), (shards_of,), jnp.float32, least / len(shards), high / len(shards))
        return jnp.repeat(jnp.exp(draws), extent[position] // shards_of).reshape((-1,) + (1,) * (len(extent) - position - 1))

    level = one(*shards[0])
    for cut in shards[1:]:
        level = level * one(*cut)
    return level


def centred(stream_key, shape, scale, limit, pieces=(), dtype=jnp.bfloat16):
    gain = steps_of(stream_key, shape, pieces, -0.22, 0.18) if pieces else 1.0
    result = jax.random.normal(stream_key, shape, jnp.float32) * scale * gain
    return jnp.minimum(jnp.maximum(result, -limit), limit).astype(dtype)


def setup_inputs(seed: int = 0, part: int = 0) -> dict:
    splits = jax.random.split(jax.random.key(seed), 6)
    part_keys = jax.random.split(jax.random.fold_in(splits[5], part), 6)
    states = centred(part_keys[0], (STREAMS, D), 1.0, 6.0, ((0, 8), (1, 2)), jnp.float32)
    norm_gain = jnp.clip(1.0 + 0.15 * jax.random.normal(splits[1], (D,), jnp.float32), 0.25, 1.75)
    gate_weight = centred(splits[2], (D, FF), D ** -0.5, 0.0625, ((0, 2), (1, 8)))
    up_weight = centred(splits[3], (D, FF), D ** -0.5, 0.0625, ((0, 2), (1, 8)))
    down_weight = centred(splits[4], (FF, D), FF ** -0.5, 0.046875, ((0, 8), (1, 2)))
    return {"states": states, "norm_gain": norm_gain, "gate_weight": gate_weight, "up_weight": up_weight, "down_weight": down_weight}


def reference(states, norm_gain, gate_weight, up_weight, down_weight):
    power = lax.optimization_barrier(jnp.mean(states * states, axis=1, keepdims=True))
    normed = (states * norm_gain[None, :] * jax.lax.rsqrt(power + 1e-05)).astype(jnp.bfloat16)
    gate = jnp.dot(normed, gate_weight, preferred_element_type=jnp.float32)
    up = jnp.dot(normed, up_weight, preferred_element_type=jnp.float32)
    hidden = (jax.nn.silu(gate) * up).astype(jnp.bfloat16)
    return states + jnp.dot(hidden, down_weight, preferred_element_type=jnp.float32)
```

```python
import functools

import jax
import jax.numpy as jnp
from jax import lax
from jax.experimental import pallas as pl
from jax.experimental.pallas import tpu as pltpu
from jax.sharding import PartitionSpec as P

MESH = pl.DeviceIdType.MESH
F32 = jnp.float32
BF16 = jnp.bfloat16
GATHER_CHUNKS = 4
DOWN_CHUNKS = 4
WIDTH = 512


def kernel(
    n, features, states, gain, gate_hbm, up_hbm, down_hbm, out,
    gate_w, up_w, down_w, x_own, x_all, pow_own, pow_all, pow_mine, pow_other,
    part, part_other, hidden, y_part, y_all,
    w_sem, d_sem, x_send, x_recv, p_send, p_recv, q_send, q_recv, e_send, e_recv, y_send, y_recv,
):
    me = lax.axis_index("hid")
    core = lax.axis_index("wid")
    partner = {"wid": 1 - core}
    chunks, depth, _ = gate_w.shape
    cols, _, span = down_w.shape
    blocks, _, streams, width = part.shape
    rows = states.shape[0]

    barrier = pltpu.get_barrier_semaphore()

    def every_peer(body):
        def step(offset, carry):
            body(lax.rem(me + offset, n))
            return carry

        lax.fori_loop(1, n, step, 0, unroll=n <= 8)

    def greet(peer):
        pl.semaphore_signal(barrier, inc=1, device_id={"hid": peer}, device_id_type=MESH)

    every_peer(greet)
    pl.semaphore_signal(barrier, inc=1, device_id=partner, device_id_type=MESH)

    def gate_copy(c):
        return pltpu.make_async_copy(gate_hbm.at[pl.ds(c * depth, depth)], gate_w.at[c], w_sem.at[0, c])

    def up_copy(c):
        return pltpu.make_async_copy(up_hbm.at[pl.ds(c * depth, depth)], up_w.at[c], w_sem.at[1, c])

    def down_copy(j):
        return pltpu.make_async_copy(down_hbm.at[:, pl.ds(j * span, span)], down_w.at[j], d_sem.at[j])

    for c in range(chunks):
        gate_copy(c).start()
        up_copy(c).start()
    for j in range(cols):
        down_copy(j).start()

    power = jnp.zeros((rows, 1), F32)
    for c in range(chunks):
        piece = states[:, c * depth:(c + 1) * depth]
        power = power + jnp.sum(piece * piece, axis=1, keepdims=True)
        scaled = (piece * gain[:, c * depth:(c + 1) * depth]).astype(BF16)
        x_own[c] = scaled
        x_all[c, me] = scaled
    power = jnp.broadcast_to(power, (rows, 128))
    pow_own[...] = power
    pow_all[me] = power

    pl.semaphore_wait(barrier, n)

    def send_x(c):
        def one(peer):
            pltpu.make_async_remote_copy(
                src_ref=x_own.at[c], dst_ref=x_all.at[c, me],
                send_sem=x_send.at[c], recv_sem=x_recv.at[c],
                device_id={"hid": peer}, device_id_type=MESH,
            ).start()

        every_peer(one)

    def send_power(peer):
        pltpu.make_async_remote_copy(
            src_ref=pow_own, dst_ref=pow_all.at[me],
            send_sem=p_send, recv_sem=p_recv,
            device_id={"hid": peer}, device_id_type=MESH,
        ).start()

    for c in range(chunks):
        send_x(c)
    every_peer(send_power)

    def wait_bytes(ref, sem):
        pltpu.make_async_copy(ref, ref, sem).wait()

    def exchange(b):
        return pltpu.make_async_remote_copy(
            src_ref=part.at[b], dst_ref=part_other.at[b],
            send_sem=e_send.at[b], recv_sem=e_recv.at[b],
            device_id=partner, device_id_type=MESH,
        )

    swap_power = pltpu.make_async_remote_copy(
        src_ref=pow_mine, dst_ref=pow_other, send_sem=q_send, recv_sem=q_recv,
        device_id=partner, device_id_type=MESH,
    )

    for c in range(chunks):
        wait_bytes(x_all.at[c, pl.ds(0, n - 1)], x_recv.at[c])
        x = x_all[c].reshape(streams, depth)
        gate_copy(c).wait()
        up_copy(c).wait()
        if c == chunks - 1:
            wait_bytes(pow_all.at[pl.ds(0, n - 1)], p_recv)
            pow_mine[...] = pow_all[...].reshape(streams, 128)
            swap_power.start()
        for b in range(blocks):
            for which, weight in ((0, gate_w), (1, up_w)):
                product = jnp.dot(x, weight[c, :, b * width:(b + 1) * width], preferred_element_type=F32)
                if c == 0:
                    part[b, which] = product
                else:
                    part[b, which] += product
            if c == chunks - 1:
                exchange(b).start()

    swap_power.wait_recv()
    mean = (pow_mine[:, :1] + pow_other[:, :1]) / features
    scale = lax.rsqrt(mean + 1e-5)
    for b in range(blocks):
        exchange(b).wait_recv()
        gate = (part[b, 0] + part_other[b, 0]) * scale
        up = (part[b, 1] + part_other[b, 1]) * scale
        hidden[:, b * width:(b + 1) * width] = (gate / (1.0 + jnp.exp(-gate)) * up).astype(BF16)

    h = hidden[...]
    step = min(span, WIDTH)
    for j in range(cols):
        down_copy(j).wait()
        for s in range(0, span, step):
            y = jnp.dot(h, down_w[j, :, s:s + step], preferred_element_type=F32)
            y_part[j, :, :, s:s + step] = y.reshape(n, rows, step).astype(BF16)
        y_all[j, me] = y_part[j, me]

        def send_y(peer):
            pltpu.make_async_remote_copy(
                src_ref=y_part.at[j, peer], dst_ref=y_all.at[j, me],
                send_sem=y_send.at[j], recv_sem=y_recv.at[j],
                device_id={"hid": peer}, device_id_type=MESH,
            ).start()

        every_peer(send_y)

    for j in range(cols):
        wait_bytes(y_all.at[j, pl.ds(0, n - 1)], y_recv.at[j])
        total = jnp.sum(y_all[j].astype(F32), axis=0)
        out[:, j * span:(j + 1) * span] = states[:, j * span:(j + 1) * span] + total

    for c in range(chunks):
        wait_bytes(x_all.at[c, pl.ds(0, n - 1)], x_send.at[c])
    wait_bytes(pow_all.at[pl.ds(0, n - 1)], p_send)
    swap_power.wait_send()
    for b in range(blocks):
        exchange(b).wait_send()
    for j in range(cols):
        wait_bytes(y_part.at[j, pl.ds(0, n - 1)], y_send.at[j])


def solution(mesh):
    n = mesh.shape["hid"]

    def local(states, norm_gain, gate_weight, up_weight, down_weight):
        rows, half = states.shape
        units = gate_weight.shape[1]
        streams = rows * n
        chunks, cols = GATHER_CHUNKS, DOWN_CHUNKS
        depth, span = half // chunks, half // cols
        width = min(WIDTH, units)
        blocks = units // width
        dma = pltpu.SemaphoreType.DMA
        return pl.pallas_call(
            functools.partial(kernel, n, half * mesh.shape["wid"]),
            out_shape=jax.ShapeDtypeStruct((rows, half), F32),
            in_specs=[pl.BlockSpec(memory_space=pltpu.VMEM)] * 2 + [pl.BlockSpec(memory_space=pl.ANY)] * 3,
            out_specs=pl.BlockSpec(memory_space=pltpu.VMEM),
            scratch_shapes=[
                pltpu.VMEM((chunks, depth, units), BF16),
                pltpu.VMEM((chunks, depth, units), BF16),
                pltpu.VMEM((cols, units, span), BF16),
                pltpu.VMEM((chunks, rows, depth), BF16),
                pltpu.VMEM((chunks, n, rows, depth), BF16),
                pltpu.VMEM((rows, 128), F32),
                pltpu.VMEM((n, rows, 128), F32),
                pltpu.VMEM((streams, 128), F32),
                pltpu.VMEM((streams, 128), F32),
                pltpu.VMEM((blocks, 2, streams, width), F32),
                pltpu.VMEM((blocks, 2, streams, width), F32),
                pltpu.VMEM((streams, units), BF16),
                pltpu.VMEM((cols, n, rows, span), BF16),
                pltpu.VMEM((cols, n, rows, span), BF16),
                dma((2, chunks)),
                dma((cols,)),
                dma((chunks,)),
                dma((chunks,)),
                dma(()),
                dma(()),
                dma(()),
                dma(()),
                dma((blocks,)),
                dma((blocks,)),
                dma((cols,)),
                dma((cols,)),
            ],
            compiler_params=pltpu.CompilerParams(
                collective_id=0, has_side_effects=True, vmem_limit_bytes=67043328
            ),
        )(states, norm_gain.reshape(1, half), gate_weight, up_weight, down_weight)

    return jax.shard_map(
        local,
        mesh=mesh,
        in_specs=(
            P(("rep", "hid"), "wid"),
            P("wid"),
            P("wid", "hid"),
            P("wid", "hid"),
            P("hid", "wid"),
        ),
        out_specs=P(("rep", "hid"), "wid"),
        check_vma=False,
    )
```

```python
import functools

import jax
import jax.numpy as jnp
from jax import lax
from jax.experimental import pallas as pl
from jax.experimental.pallas import tpu as pltpu
from jax.sharding import PartitionSpec as P

MESH = pl.DeviceIdType.MESH
F32 = jnp.float32
BF16 = jnp.bfloat16
GATHER_CHUNKS = 4
WEIGHT_CHUNKS = 8
DOWN_CHUNKS = 8
AHEAD = 3
FIRST = 3
MIDDLE = 4
WIDTH = 512


def kernel(
    n, features, states_hbm, gain_hbm, gate_hbm, up_hbm, down_hbm, out,
    states, gain, gate_w, up_w, down_w, scaled, x_own, x_all, pow_own, pow_other,
    part, part_other, hidden, y_part, y_all,
    in_sem, w_sem, d_sem, x_send, x_recv, p_send, p_recv, e_send, e_recv, y_send, y_recv,
):
    me = lax.axis_index("hid")
    core = lax.axis_index("wid")
    partner = {"wid": 1 - core}
    steps, depth, _ = gate_w.shape
    chunks, _, piece = x_own.shape
    cols, _, span = down_w.shape
    blocks, _, streams, width = part.shape
    rows = states.shape[0]

    barrier = pltpu.get_barrier_semaphore()

    def every_peer(body):
        def step(offset, carry):
            body(lax.rem(me + offset, n))
            return carry

        lax.fori_loop(1, n, step, 0, unroll=n <= 8)

    def greet(peer):
        pl.semaphore_signal(barrier, inc=1, device_id={"hid": peer}, device_id_type=MESH)

    every_peer(greet)
    pl.semaphore_signal(barrier, inc=1, device_id=partner, device_id_type=MESH)

    load_states = pltpu.make_async_copy(states_hbm, states, in_sem.at[0])
    load_gain = pltpu.make_async_copy(gain_hbm, gain, in_sem.at[1])
    load_states.start()
    load_gain.start()

    def gate_copy(c):
        return pltpu.make_async_copy(gate_hbm.at[pl.ds(c * depth, depth)], gate_w.at[c], w_sem.at[0, c])

    def up_copy(c):
        return pltpu.make_async_copy(up_hbm.at[pl.ds(c * depth, depth)], up_w.at[c], w_sem.at[1, c])

    def down_copy(j):
        return pltpu.make_async_copy(down_hbm.at[:, pl.ds(j * span, span)], down_w.at[j], d_sem.at[j])

    def start_weights(first, last):
        for c in range(first, last):
            gate_copy(c).start()
            up_copy(c).start()

    start_weights(0, FIRST)

    load_states.wait()
    load_gain.wait()
    power = jnp.zeros((rows, 1), F32)
    for c in range(chunks):
        here = slice(c * piece, (c + 1) * piece)
        value = states[:, here]
        power = power + jnp.sum(value * value, axis=1, keepdims=True)
        scaled[:, here] = value * gain[:, here]
    pow_own[...] = jnp.broadcast_to(power, (rows, 128))

    pl.semaphore_wait(barrier, n)

    swap_power = pltpu.make_async_remote_copy(
        src_ref=pow_own, dst_ref=pow_other, send_sem=p_send, recv_sem=p_recv,
        device_id=partner, device_id_type=MESH,
    )
    swap_power.start()

    def wait_bytes(ref, sem):
        pltpu.make_async_copy(ref, ref, sem).wait()

    def exchange(b):
        return pltpu.make_async_remote_copy(
            src_ref=part.at[b], dst_ref=part_other.at[b],
            send_sem=e_send.at[b], recv_sem=e_recv.at[b],
            device_id=partner, device_id_type=MESH,
        )

    start_weights(FIRST, MIDDLE)
    swap_power.wait_recv()
    scale = lax.rsqrt((pow_own[:, :1] + pow_other[:, :1]) / features + 1e-5)
    for c in range(chunks):
        x_own[c] = (scaled[:, c * piece:(c + 1) * piece] * scale).astype(BF16)

        def send_x(peer):
            pltpu.make_async_remote_copy(
                src_ref=x_own.at[c], dst_ref=x_all.at[c, me],
                send_sem=x_send.at[c], recv_sem=x_recv.at[c],
                device_id={"hid": peer}, device_id_type=MESH,
            ).start()

        every_peer(send_x)
        x_all[c, me] = x_own[c]

    start_weights(MIDDLE, steps)
    for j in range(min(AHEAD, cols)):
        down_copy(j).start()

    for c in range(steps):
        whole, inner = divmod(c * depth, piece)
        if inner == 0:
            wait_bytes(x_all.at[whole, pl.ds(0, n - 1)], x_recv.at[whole])
        x = x_all[whole, :, :, inner:inner + depth].reshape(streams, depth)
        gate_copy(c).wait()
        up_copy(c).wait()
        for b in range(blocks):
            for which, weight in ((0, gate_w), (1, up_w)):
                product = jnp.dot(x, weight[c, :, b * width:(b + 1) * width], preferred_element_type=F32)
                if c == 0:
                    part[b, which] = product
                else:
                    part[b, which] += product
            if c == steps - 1:
                exchange(b).start()

    for j in range(cols):
        down_copy(j).wait()
        if j + AHEAD < cols:
            down_copy(j + AHEAD).start()
        if j == 0:
            y = jnp.zeros((streams, span), F32)
            for b in range(blocks):
                exchange(b).wait_recv()
                gate = part[b, 0] + part_other[b, 0]
                up = part[b, 1] + part_other[b, 1]
                h = (gate / (1.0 + jnp.exp(-gate)) * up).astype(BF16)
                hidden[:, b * width:(b + 1) * width] = h
                y = y + jnp.dot(h, down_w[j, b * width:(b + 1) * width, :], preferred_element_type=F32)
        else:
            y = jnp.dot(hidden[...], down_w[j], preferred_element_type=F32)
        y_part[j] = y.reshape(n, rows, span).astype(BF16)

        def send_y(peer):
            pltpu.make_async_remote_copy(
                src_ref=y_part.at[j, peer], dst_ref=y_all.at[j, me],
                send_sem=y_send.at[j], recv_sem=y_recv.at[j],
                device_id={"hid": peer}, device_id_type=MESH,
            ).start()

        every_peer(send_y)
        y_all[j, me] = y_part[j, me]

    for j in range(cols):
        wait_bytes(y_all.at[j, pl.ds(0, n - 1)], y_recv.at[j])
        total = jnp.sum(y_all[j].astype(F32), axis=0)
        out[:, j * span:(j + 1) * span] = states[:, j * span:(j + 1) * span] + total

    for c in range(chunks):
        wait_bytes(x_all.at[c, pl.ds(0, n - 1)], x_send.at[c])
    swap_power.wait_send()
    for b in range(blocks):
        exchange(b).wait_send()
    for j in range(cols):
        wait_bytes(y_part.at[j, pl.ds(0, n - 1)], y_send.at[j])


def solution(mesh):
    n = mesh.shape["hid"]

    def local(states, norm_gain, gate_weight, up_weight, down_weight):
        rows, half = states.shape
        units = gate_weight.shape[1]
        streams = rows * n
        chunks, steps, cols = GATHER_CHUNKS, WEIGHT_CHUNKS, DOWN_CHUNKS
        piece, depth, span = half // chunks, half // steps, half // cols
        width = min(WIDTH, units)
        blocks = units // width
        dma = pltpu.SemaphoreType.DMA
        return pl.pallas_call(
            functools.partial(kernel, n, half * mesh.shape["wid"]),
            out_shape=jax.ShapeDtypeStruct((rows, half), F32),
            in_specs=[pl.BlockSpec(memory_space=pl.ANY)] * 5,
            out_specs=pl.BlockSpec(memory_space=pltpu.VMEM),
            scratch_shapes=[
                pltpu.VMEM((rows, half), F32),
                pltpu.VMEM((1, half), F32),
                pltpu.VMEM((steps, depth, units), BF16),
                pltpu.VMEM((steps, depth, units), BF16),
                pltpu.VMEM((cols, units, span), BF16),
                pltpu.VMEM((rows, half), F32),
                pltpu.VMEM((chunks, rows, piece), BF16),
                pltpu.VMEM((chunks, n, rows, piece), BF16),
                pltpu.VMEM((rows, 128), F32),
                pltpu.VMEM((rows, 128), F32),
                pltpu.VMEM((blocks, 2, streams, width), F32),
                pltpu.VMEM((blocks, 2, streams, width), F32),
                pltpu.VMEM((streams, units), BF16),
                pltpu.VMEM((cols, n, rows, span), BF16),
                pltpu.VMEM((cols, n, rows, span), BF16),
                dma((2,)),
                dma((2, steps)),
                dma((cols,)),
                dma((chunks,)),
                dma((chunks,)),
                dma(()),
                dma(()),
                dma((blocks,)),
                dma((blocks,)),
                dma((cols,)),
                dma((cols,)),
            ],
            compiler_params=pltpu.CompilerParams(
                collective_id=0, has_side_effects=True, vmem_limit_bytes=67043328
            ),
        )(states, norm_gain.reshape(1, half), gate_weight, up_weight, down_weight)

    return jax.shard_map(
        local,
        mesh=mesh,
        in_specs=(
            P(("rep", "hid"), "wid"),
            P("wid"),
            P("wid", "hid"),
            P("wid", "hid"),
            P("hid", "wid"),
        ),
        out_specs=P(("rep", "hid"), "wid"),
        check_vma=False,
    )
```

```python
import functools

import jax
import jax.numpy as jnp
from jax import lax
from jax.experimental import pallas as pl
from jax.experimental.pallas import tpu as pltpu
from jax.sharding import PartitionSpec as P

MESH = pl.DeviceIdType.MESH
F32 = jnp.float32
BF16 = jnp.bfloat16
GATHER_CHUNKS = 4
WEIGHT_CHUNKS = 8
DOWN_CHUNKS = 4
AHEAD = 2
FIRST = 3
MIDDLE = 4
WIDTH = 512


def kernel(
    n, features, states_hbm, gain_hbm, gate_hbm, up_hbm, down_hbm, out,
    states, gain, gate_w, up_w, down_w, scaled, x_own, x_all, pow_own, pow_other,
    part, part_other, hidden, y_part, y_all,
    in_sem, w_sem, d_sem, x_send, x_recv, p_send, p_recv, e_send, e_recv, y_send, y_recv,
):
    me = lax.axis_index("hid")
    core = lax.axis_index("wid")
    partner = {"wid": 1 - core}
    steps, depth, _ = gate_w.shape
    chunks, _, piece = x_own.shape
    cols, _, span = down_w.shape
    blocks, _, streams, width = part.shape
    rows = states.shape[0]

    barrier = pltpu.get_barrier_semaphore()

    def every_peer(body):
        def step(offset, carry):
            body(lax.rem(me + offset, n))
            return carry

        lax.fori_loop(1, n, step, 0, unroll=n <= 8)

    def greet(peer):
        pl.semaphore_signal(barrier, inc=1, device_id={"hid": peer}, device_id_type=MESH)

    every_peer(greet)
    pl.semaphore_signal(barrier, inc=1, device_id=partner, device_id_type=MESH)

    load_states = pltpu.make_async_copy(states_hbm, states, in_sem.at[0])
    load_gain = pltpu.make_async_copy(gain_hbm, gain, in_sem.at[1])
    load_states.start()
    load_gain.start()

    def gate_copy(c):
        return pltpu.make_async_copy(gate_hbm.at[pl.ds(c * depth, depth)], gate_w.at[c], w_sem.at[0, c])

    def up_copy(c):
        return pltpu.make_async_copy(up_hbm.at[pl.ds(c * depth, depth)], up_w.at[c], w_sem.at[1, c])

    def down_copy(j):
        return pltpu.make_async_copy(down_hbm.at[:, pl.ds(j * span, span)], down_w.at[j], d_sem.at[j])

    def start_weights(first, last):
        for c in range(first, last):
            gate_copy(c).start()
            up_copy(c).start()

    start_weights(0, FIRST)

    load_states.wait()
    load_gain.wait()
    power = jnp.zeros((rows, 1), F32)
    for c in range(chunks):
        here = slice(c * piece, (c + 1) * piece)
        value = states[:, here]
        power = power + jnp.sum(value * value, axis=1, keepdims=True)
        scaled[:, here] = value * gain[:, here]
    pow_own[...] = jnp.broadcast_to(power, (rows, 128))

    pl.semaphore_wait(barrier, n)

    swap_power = pltpu.make_async_remote_copy(
        src_ref=pow_own, dst_ref=pow_other, send_sem=p_send, recv_sem=p_recv,
        device_id=partner, device_id_type=MESH,
    )
    swap_power.start()

    def wait_bytes(ref, sem):
        pltpu.make_async_copy(ref, ref, sem).wait()

    def exchange(b):
        return pltpu.make_async_remote_copy(
            src_ref=part.at[b], dst_ref=part_other.at[b],
            send_sem=e_send.at[b], recv_sem=e_recv.at[b],
            device_id=partner, device_id_type=MESH,
        )

    start_weights(FIRST, MIDDLE)
    swap_power.wait_recv()
    scale = lax.rsqrt((pow_own[:, :1] + pow_other[:, :1]) / features + 1e-5)
    for c in range(chunks):
        x_own[c] = (scaled[:, c * piece:(c + 1) * piece] * scale).astype(BF16)

        def send_x(peer):
            pltpu.make_async_remote_copy(
                src_ref=x_own.at[c], dst_ref=x_all.at[c, me],
                send_sem=x_send.at[c], recv_sem=x_recv.at[c],
                device_id={"hid": peer}, device_id_type=MESH,
            ).start()

        every_peer(send_x)
        x_all[c, me] = x_own[c]

    start_weights(MIDDLE, steps)
    for j in range(min(AHEAD, cols)):
        down_copy(j).start()

    for c in range(steps):
        whole, inner = divmod(c * depth, piece)
        if inner == 0:
            wait_bytes(x_all.at[whole, pl.ds(0, n - 1)], x_recv.at[whole])
        x = x_all[whole, :, :, inner:inner + depth].reshape(streams, depth)
        gate_copy(c).wait()
        up_copy(c).wait()
        for b in range(blocks):
            for which, weight in ((0, gate_w), (1, up_w)):
                product = jnp.dot(x, weight[c, :, b * width:(b + 1) * width], preferred_element_type=F32)
                if c == 0:
                    part[b, which] = product
                else:
                    part[b, which] += product
            if c == steps - 1:
                exchange(b).start()

    for j in range(cols):
        down_copy(j).wait()
        if j + AHEAD < cols:
            down_copy(j + AHEAD).start()
        if j == 0:
            y = jnp.zeros((streams, span), F32)
            for b in range(blocks):
                exchange(b).wait_recv()
                gate = part[b, 0] + part_other[b, 0]
                up = part[b, 1] + part_other[b, 1]
                h = (gate / (1.0 + jnp.exp(-gate)) * up).astype(BF16)
                hidden[:, b * width:(b + 1) * width] = h
                y = y + jnp.dot(h, down_w[j, b * width:(b + 1) * width, :], preferred_element_type=F32)
        else:
            y = jnp.dot(hidden[...], down_w[j], preferred_element_type=F32)
        y_part[j] = y.reshape(n, rows, span).astype(BF16)

        def send_y(peer):
            pltpu.make_async_remote_copy(
                src_ref=y_part.at[j, peer], dst_ref=y_all.at[j, me],
                send_sem=y_send.at[j], recv_sem=y_recv.at[j],
                device_id={"hid": peer}, device_id_type=MESH,
            ).start()

        every_peer(send_y)
        y_all[j, me] = y_part[j, me]

    for j in range(cols):
        wait_bytes(y_all.at[j, pl.ds(0, n - 1)], y_recv.at[j])
        total = jnp.sum(y_all[j].astype(F32), axis=0)
        out[:, j * span:(j + 1) * span] = states[:, j * span:(j + 1) * span] + total

    for c in range(chunks):
        wait_bytes(x_all.at[c, pl.ds(0, n - 1)], x_send.at[c])
    swap_power.wait_send()
    for b in range(blocks):
        exchange(b).wait_send()
    for j in range(cols):
        wait_bytes(y_part.at[j, pl.ds(0, n - 1)], y_send.at[j])


def solution(mesh):
    n = mesh.shape["hid"]

    def local(states, norm_gain, gate_weight, up_weight, down_weight):
        rows, half = states.shape
        units = gate_weight.shape[1]
        streams = rows * n
        chunks, steps, cols = GATHER_CHUNKS, WEIGHT_CHUNKS, DOWN_CHUNKS
        piece, depth, span = half // chunks, half // steps, half // cols
        width = min(WIDTH, units)
        blocks = units // width
        dma = pltpu.SemaphoreType.DMA
        return pl.pallas_call(
            functools.partial(kernel, n, half * mesh.shape["wid"]),
            out_shape=jax.ShapeDtypeStruct((rows, half), F32),
            in_specs=[pl.BlockSpec(memory_space=pl.ANY)] * 5,
            out_specs=pl.BlockSpec(memory_space=pltpu.VMEM),
            scratch_shapes=[
                pltpu.VMEM((rows, half), F32),
                pltpu.VMEM((1, half), F32),
                pltpu.VMEM((steps, depth, units), BF16),
                pltpu.VMEM((steps, depth, units), BF16),
                pltpu.VMEM((cols, units, span), BF16),
                pltpu.VMEM((rows, half), F32),
                pltpu.VMEM((chunks, rows, piece), BF16),
                pltpu.VMEM((chunks, n, rows, piece), BF16),
                pltpu.VMEM((rows, 128), F32),
                pltpu.VMEM((rows, 128), F32),
                pltpu.VMEM((blocks, 2, streams, width), F32),
                pltpu.VMEM((blocks, 2, streams, width), F32),
                pltpu.VMEM((streams, units), BF16),
                pltpu.VMEM((cols, n, rows, span), BF16),
                pltpu.VMEM((cols, n, rows, span), BF16),
                dma((2,)),
                dma((2, steps)),
                dma((cols,)),
                dma((chunks,)),
                dma((chunks,)),
                dma(()),
                dma(()),
                dma((blocks,)),
                dma((blocks,)),
                dma((cols,)),
                dma((cols,)),
            ],
            compiler_params=pltpu.CompilerParams(
                collective_id=0, has_side_effects=True, vmem_limit_bytes=67043328
            ),
        )(states, norm_gain.reshape(1, half), gate_weight, up_weight, down_weight)

    return jax.shard_map(
        local,
        mesh=mesh,
        in_specs=(
            P(("rep", "hid"), "wid"),
            P("wid"),
            P("wid", "hid"),
            P("wid", "hid"),
            P("hid", "wid"),
        ),
        out_specs=P(("rep", "hid"), "wid"),
        check_vma=False,
    )
```
